128 devices in a mesh: pos: 16 (over y, z), tile: 8 (over x, core).
Axes of the slice: x: 4, y: 4, z: 4, core: 2. Of those that a mesh axis runs over, the one named last changes fastest.
Arguments:
- object_slices: float32 [2, 2, 4096, 2048], P(None, None, 'pos', 'tile'), may hold values from -4.2 to 4.2
- probe: float32 [2, 256, 256], replicated, may hold values from -6 to 6
- amplitudes: float32 [16, 8, 8, 256, 256], P('pos', 'tile'), may hold values from 0 to 2
- offsets: int32 [16, 8, 8, 2], P('pos', 'tile'), may hold values from -128 to 127, as said below
- counts: int32 [16, 8], P('pos', 'tile'), may hold values from 1 to 8, as said below
Outputs:
- object_grad: float32 [2, 2, 4096, 2048], P(None, None, 'pos', 'tile')
- probe_grad: float32 [2, 256, 256], replicated
The draws below stay inside these ranges and needn't reach their ends.
Inputs may be any that keep to these rules, and one draw needn't show every extreme that they name: Every patch lies inside the object: offsets are -128 to 127, and 0 or more on the first row or column of tiles, 0 or less on the last. `counts`: some tile has 8 live slots and some tile has one.
All inputs are finite; a program needn't handle non-finite values.
Results may differ from the reference program's by a relative error of at most 0.0003.
Values sent between devices are 32-bit elements; how exact they have to be, the bound alone decides.
No kernel may reach another device: no remote copies, remote signals or barrier semaphores. Data moves between devices by JAX's collectives and lax.ppermute only.
A program may use at most 64 MiB of HBM per device.

```python
import jax
import jax.numpy as jnp
from jax import lax

PAT = 256
HALF = 128
SLICES = 2
CAP = 8
GRID_ROWS = 16
GRID_COLS = 8
OBJ_ROWS = 4096
OBJ_COLS = 2048


def draw_offsets(key, part):
    raw = jax.random.randint(key, (GRID_ROWS, GRID_COLS, CAP, 2), -HALF, HALF)
    rows = jnp.arange(GRID_ROWS)[:, None, None]
    cols = jnp.arange(GRID_COLS)[None, :, None]
    low_y = jnp.where(rows == 0, 0, -HALF)
    high_y = jnp.where(rows == GRID_ROWS - 1, 0, HALF - 1)
    low_x = jnp.where(cols == 0, 0, -HALF)
    high_x = jnp.where(cols == GRID_COLS - 1, 0, HALF - 1)
    down = jnp.clip(raw[..., 0], low_y, high_y)
    across = jnp.clip(raw[..., 1], low_x, high_x)
    return jnp.stack([down, across], axis=-1).astype(jnp.int32)


def draw_counts(key, part):
    number = GRID_ROWS * GRID_COLS
    base = jax.random.randint(key, (number,), 1, CAP + 1)
    first = jax.random.randint(jax.random.fold_in(key, 11), (), 0, number)
    step = jax.random.randint(jax.random.fold_in(key, 13), (), 1, number)
    second = (first + step) % number
    places = jnp.arange(number)
    base = jnp.where(places == first, CAP, base)
    base = jnp.where(places == second, 1, base)
    return base.reshape(GRID_ROWS, GRID_COLS).astype(jnp.int32)


def levels(key, dims, pieces, smallest, top_value):
    def one(axis_at, blocks):
        draws = jax.random.uniform(jax.random.fold_in(jax.random.fold_in(key, 6), axis_at), (blocks,), jnp.float32, smallest / len(pieces), top_value / len(pieces))
        return jnp.repeat(jnp.exp(draws), dims[axis_at] // blocks).reshape((-1,) + (1,) * (len(dims) - axis_at - 1))

    factor_of = one(*pieces[0])
    for cut in pieces[1:]:
        factor_of = factor_of * one(*cut)
    return factor_of


def normal_values(rng, dims, width, reach, shards=(), kind=jnp.bfloat16):
    values = jax.random.normal(rng, dims, jnp.float32) * width
    if len(shards) > 0:
        values = levels(rng, dims, shards, -0.22, 0.18) * values
    return jnp.clip(values, min=-reach, max=reach).astype(kind)


def setup_inputs(seed: int = 0) -> dict:
    keys = jax.random.split(jax.random.key(seed), 6)
    object_slices = normal_values(keys[0], (SLICES, 2, OBJ_ROWS, OBJ_COLS), 0.7, 4.2, ((2, 16), (3, 8)), jnp.float32)
    probe = normal_values(keys[1], (2, PAT, PAT), 1.0, 6.0, (), jnp.float32)
    amplitudes = jnp.clip(2.0 * jax.random.uniform(keys[2], (GRID_ROWS, GRID_COLS, CAP, PAT, PAT), jnp.float32) ** levels(keys[2], (GRID_ROWS, GRID_COLS, CAP, PAT, PAT), ((0, 16), (1, 8)), -0.2, 0.2), 0.0, 2.0)
    offsets = draw_offsets(jax.random.fold_in(keys[5], 71), 0)
    counts = draw_counts(jax.random.fold_in(keys[5], 71), 0)
    return {"object_slices": object_slices, "probe": probe, "amplitudes": amplitudes, "offsets": offsets, "counts": counts}


def position_loss(patch, probe, amp, kernel):
    psi = lax.complex(probe[0], probe[1])
    for slab in range(SLICES):
        psi = psi * lax.complex(patch[slab, 0], patch[slab, 1])
        if slab < SLICES - 1:
            psi = jnp.fft.ifft2(jnp.fft.fft2(psi) * kernel)
    far = jnp.fft.fft2(psi, norm='ortho')
    magnitude = jnp.sqrt(jnp.real(far) ** 2 + jnp.imag(far) ** 2 + 0.01)
    return jnp.sum((magnitude - amp) ** 2)

def reference(object_slices, probe, amplitudes, offsets, counts):
    freq = jnp.fft.fftfreq(PAT) * PAT
    phase = -(80.0 / (PAT * PAT)) * (freq[:, None] ** 2 + freq[None, :] ** 2)
    kernel = lax.complex(jnp.cos(phase), jnp.sin(phase))
    total = GRID_ROWS * GRID_COLS * CAP
    flat_offsets = offsets.reshape(total, 2)
    flat_amps = amplitudes.reshape(total, PAT, PAT)
    flat_counts = counts.reshape(GRID_ROWS * GRID_COLS)
    indices = jnp.arange(total, dtype=jnp.int32)

    def visit(carry, item):
        grad, probe_grad = carry
        index, shift, amp = item
        tile_index = (index // CAP).astype(jnp.int32)
        slot = (index % CAP).astype(jnp.int32)
        row = (tile_index // GRID_COLS).astype(jnp.int32)
        col = (tile_index % GRID_COLS).astype(jnp.int32)
        top = (row * PAT + shift[0]).astype(jnp.int32)
        left = (col * PAT + shift[1]).astype(jnp.int32)
        zero = jnp.int32(0)
        live = slot < flat_counts[tile_index]
        patch = lax.dynamic_slice(object_slices, (zero, zero, top, left), (SLICES, 2, PAT, PAT))
        loss, back = jax.vjp(lambda p, q: position_loss(p, q, amp, kernel), patch, probe)
        weight = jnp.where(live, 1.0, 0.0).astype(loss.dtype)
        patch_grad, probe_term = back(weight)
        old = lax.dynamic_slice(grad, (zero, zero, top, left), (SLICES, 2, PAT, PAT))
        grad = lax.dynamic_update_slice(grad, old + patch_grad, (zero, zero, top, left))
        return ((grad, probe_grad + probe_term), None)
    start = (jnp.zeros_like(object_slices), jnp.zeros_like(probe))
    (grad, probe_grad), _ = lax.scan(visit, start, (indices, flat_offsets, flat_amps))
    return (grad, probe_grad)
```

```python
import functools
import math

import jax
import jax.numpy as jnp
import numpy as np
from jax import lax
from jax.experimental import pallas as pl
from jax.experimental.pallas import tpu as pltpu
from jax.sharding import Mesh
from jax.sharding import PartitionSpec as P

POS = ("pos_0", "pos_1")
TILE = ("tile_0", "tile_1")
CHIPS = ("pos_0", "pos_1", "tile_0")
F32 = jnp.float32
BF16 = jnp.bfloat16
ROWS = 32


def real_form(field):
    return np.block([[field.real, field.imag], [-field.imag, field.real]])


def transform_matrices(width):
    half = width // 2
    index = np.arange(width)
    signed = np.where(index < half, index, index - width)
    kernel = np.exp(-1j * 80.0 / (width * width) * signed.astype(np.float64) ** 2)
    impulse = np.fft.ifft(kernel)
    near = np.arange(half)
    gap = (near[:, None] - near[None, :]) % width
    prop_sum = 0.5 * (impulse[gap] + impulse[(gap + half) % width])
    prop_diff = 0.5 * (impulse[gap] - impulse[(gap + half) % width])
    scale = 1.0 / math.sqrt(width)
    even = np.exp(-2j * np.pi / width * (near[:, None] * (2 * near[None, :]) % width)) * scale
    odd = np.exp(-2j * np.pi / width * (near[:, None] * (2 * near[None, :] + 1) % width)) * scale
    return np.stack([real_form(m) for m in (prop_sum, prop_diff, even, odd)])


def halves(matrix):
    high = matrix.astype(np.float32).astype(BF16)
    low = (matrix - high.astype(np.float64)).astype(np.float32).astype(BF16)
    return np.stack([high, low])


def split(value):
    high = value.astype(BF16)
    low = (value - high.astype(F32)).astype(BF16)
    return high, low


def dot(left, right):
    return jnp.dot(left, right, preferred_element_type=F32)


def order_kernel(left_ref, right_ref, perm_ref, out_ref):
    half = left_ref.shape[1] // 2
    for parity in range(2):
        picked = pl.ds(parity, half, stride=2)
        rows = jnp.concatenate([left_ref[0, picked, :], right_ref[0, picked, :]], axis=1)
        first = rows.astype(BF16)
        rest = rows - first.astype(F32)
        second = rest.astype(BF16)
        third = (rest - second.astype(F32)).astype(BF16)
        perm = perm_ref[...]
        out_ref[0, parity] = dot(first, perm) + dot(second, perm) + dot(third, perm)


def ordered(amps):
    slots, width, _ = amps.shape
    index = np.arange(width)
    source = np.where(index < width // 2, 2 * index, 2 * (index - width // 2) + 1)
    perm = (index[:, None] == source[None, :]).astype(BF16)
    return pl.pallas_call(
        order_kernel,
        grid=(slots,),
        in_specs=[
            pl.BlockSpec((1, width, width // 2), lambda i: (i, 0, 0)),
            pl.BlockSpec((1, width, width // 2), lambda i: (i, 0, 1)),
            pl.BlockSpec((width, width), lambda i: (0, 0)),
        ],
        out_specs=pl.BlockSpec((1, 2, width // 2, width), lambda i: (i, 0, 0, 0)),
        out_shape=jax.ShapeDtypeStruct((slots, 2, width // 2, width), F32),
        cost_estimate=pl.CostEstimate(flops=2 * 3 * slots * width**3, bytes_accessed=8 * slots * width**2, transcendentals=0),
        name="order_amps",
    )(amps, amps, jnp.asarray(perm))


def main_kernel(
    count_ref, shift_ref, own_ref, up_ref, low_ref, left_ref, right_ref, probe_ref, amp_ref, mat_ref, matt_ref,
    g0_ref, g1_ref, g2_ref, g3_ref, probe_grad_ref,
    ext, rolled, wave, xa, wa, vv, zz, sems,
):
    half = 128
    grads = (g0_ref, g1_ref, g2_ref, g3_ref)
    copies = []
    for s in range(2):
        for c in range(2):
            for j in range(2):
                cols = pl.ds(j * half, half)
                copies.append((own_ref.at[s, c, :, cols], ext.at[1 + j, s, c, pl.ds(half, 2 * half), :]))
                copies.append((up_ref.at[s, c, :, cols], ext.at[1 + j, s, c, pl.ds(0, half), :]))
                copies.append((low_ref.at[s, c, :, cols], ext.at[1 + j, s, c, pl.ds(3 * half, half), :]))
    copies.append((left_ref, ext.at[0]))
    copies.append((right_ref, ext.at[3]))
    copies = [pltpu.make_async_copy(a, b, sems.at[n]) for n, (a, b) in enumerate(copies)]
    for copy in copies:
        copy.start()
    for g in grads:
        g[...] = jnp.zeros_like(g)
    probe_grad_ref[...] = jnp.zeros_like(probe_grad_ref)
    for copy in copies:
        copy.wait()

    lane = lax.broadcasted_iota(jnp.int32, (ROWS, half), 1)
    tiles = (pl.ds(0, half), pl.ds(half, half))

    def visit(slot, carry):
        top = shift_ref[slot, 0] + half
        left = shift_ref[slot, 1] + half
        back = lax.rem(2 * half - left, 2 * half)
        masks = (lane >= left, lane + half >= left)

        def patch(s, c, j, r):
            rows = pl.ds(top + r, ROWS)
            return jnp.where(masks[j], ext[j, s, c, rows, :], ext[j + 2, s, c, rows, :])

        def add_grad(s, c, j, r, value):
            rows = pl.ds(top + r, ROWS)
            near, far = grads[j], grads[j + 2]
            near[s, c, rows, :] = near[s, c, rows, :] + jnp.where(masks[j], value, 0.0)
            far[s, c, rows, :] = far[s, c, rows, :] + jnp.where(masks[j], 0.0, value)

        def put(ref, k, r, cols, value):
            high, low = split(value)
            ref[0, k, pl.ds(r, ROWS), cols] = high
            ref[1, k, pl.ds(r, ROWS), cols] = low

        def put_right(r, first, second):
            for c in range(2):
                put(xa, 0, r, tiles[c], first[c] + second[c])
                put(xa, 1, r, tiles[c], first[c] - second[c])

        def right(mats, base):
            for k in range(2):
                high, low = mats[0, base + k], mats[1, base + k]
                vv[k] = dot(xa[0, k], high) + dot(xa[1, k], high) + dot(xa[0, k], low)

        def left_side(mats, base):
            for k in range(2):
                high, low = mats[0, base + k], mats[1, base + k]
                zz[k] = dot(high, wa[0, k]) + dot(high, wa[1, k]) + dot(low, wa[0, k])

        def propagate(mats_right, mats_left):
            right(mats_right, 0)
            for r in range(0, half, ROWS):
                for c in range(2):
                    ts, td = vv[0, pl.ds(r, ROWS), tiles[c]], vv[1, pl.ds(r, ROWS), tiles[c]]
                    bs, bd = vv[0, pl.ds(half + r, ROWS), tiles[c]], vv[1, pl.ds(half + r, ROWS), tiles[c]]
                    sum_s, sum_d, dif_s, dif_d = ts + bs, td + bd, ts - bs, td - bd
                    put(wa, 0, c * half + r, tiles[0], sum_s + sum_d)
                    put(wa, 0, c * half + r, tiles[1], sum_s - sum_d)
                    put(wa, 1, c * half + r, tiles[0], dif_s + dif_d)
                    put(wa, 1, c * half + r, tiles[1], dif_s - dif_d)
            left_side(mats_left, 0)

        def from_left(h, r, j):
            out = []
            for c in range(2):
                a = zz[0, pl.ds(c * half + r, ROWS), tiles[j]]
                b = zz[1, pl.ds(c * half + r, ROWS), tiles[j]]
                out.append(a - b if h else a + b)
            return out

        for c in range(2):
            for r in range(0, 2 * half, ROWS):
                rolled[c, pl.ds(r, ROWS), :] = pltpu.roll(probe_ref[c, pl.ds(r, ROWS), :], left, 1)

        for r in range(0, 2 * half, ROWS):
            waves = []
            for j in range(2):
                pr, pi = (rolled[c, pl.ds(r, ROWS), tiles[j]] for c in range(2))
                re, im = (patch(0, c, j, r) for c in range(2))
                waves.append((pr * re - pi * im, pr * im + pi * re))
            put_right(r, *waves)
        propagate(mat_ref, matt_ref)
        for h in range(2):
            for r in range(0, half, ROWS):
                row = h * half + r
                waves = []
                for j in range(2):
                    wr, wi = from_left(h, r, j)
                    wave[0, pl.ds(row, ROWS), tiles[j]] = wr
                    wave[1, pl.ds(row, ROWS), tiles[j]] = wi
                    re, im = (patch(1, c, j, row) for c in range(2))
                    waves.append((wr * re - wi * im, wr * im + wi * re))
                put_right(row, *waves)
        right(mat_ref, 2)
        for r in range(0, half, ROWS):
            for c in range(2):
                for k in range(2):
                    t = vv[k, pl.ds(r, ROWS), tiles[c]]
                    b = vv[k, pl.ds(half + r, ROWS), tiles[c]]
                    put(wa, 0, c * half + r, tiles[k], t + b)
                    put(wa, 1, c * half + r, tiles[k], t - b)
        left_side(matt_ref, 2)
        for k in range(2):
            for r in range(0, half, ROWS):
                for j in range(2):
                    fr = zz[k, pl.ds(r, ROWS), tiles[j]]
                    fi = zz[k, pl.ds(half + r, ROWS), tiles[j]]
                    a = amp_ref[slot, k, pl.ds(r, ROWS), tiles[j]]
                    factor = 2.0 - 2.0 * a * lax.rsqrt(fr * fr + fi * fi + 0.01)
                    put(wa, k, r, tiles[j], factor * fr)
                    put(wa, k, half + r, tiles[j], factor * fi)
        left_side(mat_ref, 2)
        for h in range(2):
            for r in range(0, half, ROWS):
                for k in range(2):
                    gr, gi = from_left(h, r, k)
                    put(xa, k, h * half + r, tiles[0], gr)
                    put(xa, k, h * half + r, tiles[1], gi)
        right(matt_ref, 2)
        for r in range(0, 2 * half, ROWS):
            waves = []
            for j in range(2):
                grad = []
                for c in range(2):
                    a, b = vv[0, pl.ds(r, ROWS), tiles[c]], vv[1, pl.ds(r, ROWS), tiles[c]]
                    grad.append(a - b if j else a + b)
                gr, gi = grad
                wr, wi = (wave[c, pl.ds(r, ROWS), tiles[j]] for c in range(2))
                add_grad(1, 0, j, r, wr * gr + wi * gi)
                add_grad(1, 1, j, r, wr * gi - wi * gr)
                re, im = (patch(1, c, j, r) for c in range(2))
                waves.append((re * gr + im * gi, re * gi - im * gr))
            put_right(r, *waves)
        propagate(matt_ref, mat_ref)
        for h in range(2):
            for r in range(0, half, ROWS):
                row = h * half + r
                terms = ([], [])
                for j in range(2):
                    gr, gi = from_left(h, r, j)
                    pr, pi = (rolled[c, pl.ds(row, ROWS), tiles[j]] for c in range(2))
                    add_grad(0, 0, j, row, pr * gr + pi * gi)
                    add_grad(0, 1, j, row, pr * gi - pi * gr)
                    re, im = (patch(0, c, j, row) for c in range(2))
                    terms[0].append(re * gr + im * gi)
                    terms[1].append(re * gi - im * gr)
                for c in range(2):
                    term = pltpu.roll(jnp.concatenate(terms[c], axis=1), back, 1)
                    probe_grad_ref[c, pl.ds(row, ROWS), :] = probe_grad_ref[c, pl.ds(row, ROWS), :] + term
        return carry

    lax.fori_loop(0, count_ref[0, 0], visit, 0)


def gradients(count, shifts, own, up, low, left, right, probe, amps, mats, mats_t):
    width = probe.shape[-1]
    half = width // 2
    column = jax.ShapeDtypeStruct((2, 2, 4 * half, half), F32)
    any_space = pl.BlockSpec(memory_space=pl.ANY)
    vmem = pl.BlockSpec(memory_space=pltpu.VMEM)
    smem = pl.BlockSpec(memory_space=pltpu.SMEM)
    return pl.pallas_call(
        main_kernel,
        in_specs=[smem, smem] + [any_space] * 5 + [vmem] * 4,
        out_specs=[vmem] * 5,
        out_shape=[column] * 4 + [jax.ShapeDtypeStruct((2, width, width), F32)],
        scratch_shapes=[
            pltpu.VMEM((4, 2, 2, 4 * half, half), F32),
            pltpu.VMEM((2, width, width), F32),
            pltpu.VMEM((2, width, width), F32),
            pltpu.VMEM((2, 2, width, width), BF16),
            pltpu.VMEM((2, 2, width, width), BF16),
            pltpu.VMEM((2, width, width), F32),
            pltpu.VMEM((2, width, width), F32),
            pltpu.SemaphoreType.DMA((26,)),
        ],
        cost_estimate=pl.CostEstimate(flops=8 * 48 * 2 * width**3, bytes_accessed=16 << 20, transcendentals=8 * width**2),
        name="slot_gradients",
    )(count, shifts, own, up, low, left, right, probe, amps, mats, mats_t)


def from_behind(value, axis, steps):
    count = lax.axis_size(axis)
    initial, last = (max(0, -steps), min(count, count - steps))
    return lax.ppermute(value, axis, [(source, source + steps) for source in range(initial, last)])


def swap_cores(value):
    return lax.ppermute(value, "tile_1", [(0, 1), (1, 0)])


def total_over_devices(shard):
    lines = shard.reshape(-1, 128)
    count = len(lines) // 2
    first = lax.axis_index("tile_1") == 0
    send = jnp.where(first, lines[count:], lines[:count])
    own = jnp.where(first, lines[:count], lines[count:]) + swap_cores(send)
    chips = lax.axis_size(CHIPS)
    parts = lax.all_to_all(own.reshape(chips, -1, 128), CHIPS, 0, 0, tiled=True)
    mine = parts.sum(0, keepdims=True)
    spread = jnp.broadcast_to(mine, parts.shape)
    own = lax.all_to_all(spread, CHIPS, 0, 0, tiled=True).reshape(count, 128)
    other = swap_cores(own)
    whole = jnp.concatenate([jnp.where(first, own, other), jnp.where(first, other, own)])
    return whole.reshape(shard.shape)


def shards(mats, mats_t, object_slices, probe, amplitudes, offsets, counts):
    width = probe.shape[-1]
    half = width // 2
    up = from_behind(object_slices[:, :, half:], POS, 1)
    low = from_behind(object_slices[:, :, :half], POS, -1)
    tall = jnp.concatenate([up, object_slices, low], axis=2)
    left = from_behind(tall[..., half:], TILE, 1)
    right = from_behind(tall[..., :half], TILE, -1)
    amps = ordered(amplitudes[0, 0])
    g0, g1, g2, g3, probe_grad = gradients(
        counts, offsets[0, 0], object_slices, up, low, left, right, probe, amps, mats, mats_t
    )
    probe_total = total_over_devices(probe_grad)
    g1 = g1 + from_behind(g3, TILE, 1)
    g2 = g2 + from_behind(g0, TILE, -1)
    middle = jnp.concatenate([g1, g2], axis=3)
    from_above = from_behind(middle[:, :, 3 * half :], POS, 1)
    from_below = from_behind(middle[:, :, :half], POS, -1)
    object_grad = jnp.concatenate(
        [middle[:, :, half : 2 * half] + from_above, middle[:, :, 2 * half : 3 * half] + from_below], axis=2
    )
    return (object_grad, probe_total)


def solution(mesh):
    torus = Mesh(mesh.devices.reshape(4, 4, 4, 2), ("pos_0", "pos_1", "tile_0", "tile_1"))
    placed = (
        P(None, None, POS, TILE),
        P(),
        P(POS, TILE, None, None, None),
        P(POS, TILE, None, None),
        P(POS, TILE),
    )
    real = transform_matrices(256)
    mats = jnp.asarray(halves(real))
    mats_t = jnp.asarray(halves(np.swapaxes(real, 1, 2)))
    return jax.shard_map(
        functools.partial(shards, mats, mats_t),
        mesh=torus,
        in_specs=placed,
        out_specs=(P(None, None, POS, TILE), P()),
        check_vma=False,
    )
```

```python
import functools
import itertools
import math

import jax
import jax.numpy as jnp
import numpy as np
from jax import lax
from jax.experimental import pallas as pl
from jax.experimental.pallas import tpu as pltpu
from jax.sharding import Mesh
from jax.sharding import PartitionSpec as P

POS = ("pos_0", "pos_1")
TILE = ("tile_0", "tile_1")
ALL = ("pos_0", "pos_1", "tile_0", "tile_1")
F32 = jnp.float32
BF16 = jnp.bfloat16
ROWS = 32


def real_form(field):
    return np.block([[field.real, field.imag], [-field.imag, field.real]])


def transform_matrices(width):
    half = width // 2
    index = np.arange(width)
    signed = np.where(index < half, index, index - width)
    kernel = np.exp(-1j * 80.0 / (width * width) * signed.astype(np.float64) ** 2)
    impulse = np.fft.ifft(kernel)
    near = np.arange(half)
    gap = (near[:, None] - near[None, :]) % width
    prop_sum = 0.5 * (impulse[gap] + impulse[(gap + half) % width])
    prop_diff = 0.5 * (impulse[gap] - impulse[(gap + half) % width])
    scale = 1.0 / math.sqrt(width)
    even = np.exp(-2j * np.pi / width * (near[:, None] * (2 * near[None, :]) % width)) * scale
    odd = np.exp(-2j * np.pi / width * (near[:, None] * (2 * near[None, :] + 1) % width)) * scale
    return np.stack([real_form(m) for m in (prop_sum, prop_diff, even, odd)])


def halves(matrix):
    high = matrix.astype(np.float32).astype(BF16)
    low = (matrix - high.astype(np.float64)).astype(np.float32).astype(BF16)
    return np.stack([high, low])


def split(value):
    high = value.astype(BF16)
    low = (value - high.astype(F32)).astype(BF16)
    return high, low


def dot(left, right):
    return jnp.dot(left, right, preferred_element_type=F32)


def order_kernel(left_ref, right_ref, perm_ref, out_ref):
    half = left_ref.shape[1] // 2
    for parity in range(2):
        picked = pl.ds(parity, half, stride=2)
        rows = jnp.concatenate([left_ref[0, picked, :], right_ref[0, picked, :]], axis=1)
        first = rows.astype(BF16)
        rest = rows - first.astype(F32)
        second = rest.astype(BF16)
        third = (rest - second.astype(F32)).astype(BF16)
        perm = perm_ref[...]
        out_ref[0, parity] = dot(first, perm) + dot(second, perm) + dot(third, perm)


def ordered(amps):
    slots, width, _ = amps.shape
    index = np.arange(width)
    source = np.where(index < width // 2, 2 * index, 2 * (index - width // 2) + 1)
    perm = (index[:, None] == source[None, :]).astype(BF16)
    return pl.pallas_call(
        order_kernel,
        grid=(slots,),
        in_specs=[
            pl.BlockSpec((1, width, width // 2), lambda i: (i, 0, 0)),
            pl.BlockSpec((1, width, width // 2), lambda i: (i, 0, 1)),
            pl.BlockSpec((width, width), lambda i: (0, 0)),
        ],
        out_specs=pl.BlockSpec((1, 2, width // 2, width), lambda i: (i, 0, 0, 0)),
        out_shape=jax.ShapeDtypeStruct((slots, 2, width // 2, width), F32),
        cost_estimate=pl.CostEstimate(flops=2 * 3 * slots * width**3, bytes_accessed=8 * slots * width**2, transcendentals=0),
        name="order_amps",
    )(amps, amps, jnp.asarray(perm))


def main_kernel(
    count_ref, shift_ref, core_at, odd_at, own_ref, row_a_ref, row_b_ref, in_ref, out_ref, in_ends_ref, out_ends_ref, probe_ref, amps_ref, mats_ref, matts_ref,
    end_in_ref, end_out_ref, side_in_ref, side_out_ref, slab_ref, core_ref, probe_grad_ref,
    ext, gext, rolleds, waves, xas, was, vvs, zzs, amp_ref, mat_ref, matt_ref, sems, amp_sems, out_sems,
):
    half = 128
    grads = [gext.at[j] for j in range(4)]
    copies = []
    for s in range(2):
        for c in range(2):
            for j in range(2):
                copies.append((own_ref.at[s, c, :, pl.ds(j * half, half)], ext.at[1 + j, s, c, pl.ds(half, 2 * half), :]))
    middle = pl.ds(half, 2 * half)
    core, odd = core_at[0], odd_at[0]
    toward_in, toward_out = 3 * (1 - core), 3 * core
    rows_a = pl.ds(pl.multiple_of(3 * half * (1 - odd), half), half)
    rows_b = pl.ds(pl.multiple_of(3 * half * odd, half), half)
    copies.append((row_a_ref, ext.at[1:3, :, :, rows_a, :]))
    copies.append((row_b_ref, ext.at[1:3, :, :, rows_b, :]))
    for j, side, ends in ((toward_in, in_ref, in_ends_ref), (toward_out, out_ref, out_ends_ref)):
        copies.append((side, ext.at[j, :, :, middle, :]))
        copies.append((ends.at[0], ext.at[j, :, :, rows_a, :]))
        copies.append((ends.at[1], ext.at[j, :, :, rows_b, :]))
    copies = [pltpu.make_async_copy(a, b, sems.at[n]) for n, (a, b) in enumerate(copies)]
    copies.append(pltpu.make_async_copy(mats_ref, mat_ref, sems.at[len(copies)]))
    copies.append(pltpu.make_async_copy(matts_ref, matt_ref, sems.at[len(copies)]))
    for copy in copies:
        copy.start()

    def amp_copy(slot):
        return pltpu.make_async_copy(amps_ref.at[slot], amp_ref.at[slot], amp_sems.at[slot])

    for slot in range(8):
        amp_copy(slot).start()
    gext[...] = jnp.zeros_like(gext)
    probe_grad_ref[...] = jnp.zeros_like(probe_grad_ref)
    for copy in copies:
        copy.wait()

    lane = lax.broadcasted_iota(jnp.int32, (ROWS, half), 1)
    tiles = (pl.ds(0, half), pl.ds(half, half))
    count = count_ref[0, 0]

    def phases(which, slot, two):
        rolled, wave, xa, wa, vv, zz = (ref.at[which] for ref in (rolleds, waves, xas, was, vvs, zzs))
        top = shift_ref[slot, 0] + half
        left = shift_ref[slot, 1] + half
        back = lax.rem(2 * half - left, 2 * half)
        masks = (lane >= left, lane + half >= left)

        def patch(s, c, j, r):
            rows = pl.ds(top + r, ROWS)
            return jnp.where(masks[j], ext[j, s, c, rows, :], ext[j + 2, s, c, rows, :])

        def add_grad(s, c, j, r, value):
            rows = pl.ds(top + r, ROWS)
            near, far = grads[j], grads[j + 2]
            near[s, c, rows, :] = near[s, c, rows, :] + jnp.where(masks[j], value, 0.0)
            far[s, c, rows, :] = far[s, c, rows, :] + jnp.where(masks[j], 0.0, value)

        def put(ref, k, r, cols, value):
            high, low = split(value)
            ref[0, k, pl.ds(r, ROWS), cols] = high
            ref[1, k, pl.ds(r, ROWS), cols] = low

        def put_right(r, first, second):
            for c in range(2):
                put(xa, 0, r, tiles[c], first[c] + second[c])
                put(xa, 1, r, tiles[c], first[c] - second[c])

        def right(mats, base):
            def piece(k):
                high, low = mats[0, base + k], mats[1, base + k]
                vv[k] = dot(xa[0, k], high) + dot(xa[1, k], high) + dot(xa[0, k], low)

            return [functools.partial(piece, k) for k in range(2)]

        def left_side(mats, base):
            def piece(k):
                high, low = mats[0, base + k], mats[1, base + k]
                zz[k] = dot(high, wa[0, k]) + dot(high, wa[1, k]) + dot(low, wa[0, k])

            return [functools.partial(piece, k) for k in range(2)]

        def over(piece, *ranges):
            return [functools.partial(piece, *at) for at in itertools.product(*ranges)]

        upper = range(0, half, ROWS)
        all_rows = range(0, 2 * half, ROWS)

        def from_left(h, r, j):
            out = []
            for c in range(2):
                a = zz[0, pl.ds(c * half + r, ROWS), tiles[j]]
                b = zz[1, pl.ds(c * half + r, ROWS), tiles[j]]
                out.append(a - b if h else a + b)
            return out

        def start(r):
            for c in range(2):
                rolled[c, pl.ds(r, ROWS), :] = pltpu.roll(probe_ref[c, pl.ds(r, ROWS), :], left, 1)
            pair = []
            for j in range(2):
                pr, pi = (rolled[c, pl.ds(r, ROWS), tiles[j]] for c in range(2))
                re, im = (patch(0, c, j, r) for c in range(2))
                pair.append((pr * re - pi * im, pr * im + pi * re))
            put_right(r, *pair)

        def turn(r, c):
            ts, td = vv[0, pl.ds(r, ROWS), tiles[c]], vv[1, pl.ds(r, ROWS), tiles[c]]
            bs, bd = vv[0, pl.ds(half + r, ROWS), tiles[c]], vv[1, pl.ds(half + r, ROWS), tiles[c]]
            sum_s, sum_d, dif_s, dif_d = ts + bs, td + bd, ts - bs, td - bd
            put(wa, 0, c * half + r, tiles[0], sum_s + sum_d)
            put(wa, 0, c * half + r, tiles[1], sum_s - sum_d)
            put(wa, 1, c * half + r, tiles[0], dif_s + dif_d)
            put(wa, 1, c * half + r, tiles[1], dif_s - dif_d)

        def exit_wave(h, r):
            row = h * half + r
            pair = []
            for j in range(2):
                wr, wi = from_left(h, r, j)
                wave[0, pl.ds(row, ROWS), tiles[j]] = wr
                wave[1, pl.ds(row, ROWS), tiles[j]] = wi
                re, im = (patch(1, c, j, row) for c in range(2))
                pair.append((wr * re - wi * im, wr * im + wi * re))
            put_right(row, *pair)

        def turn_far(r, c):
            for k in range(2):
                t = vv[k, pl.ds(r, ROWS), tiles[c]]
                b = vv[k, pl.ds(half + r, ROWS), tiles[c]]
                put(wa, 0, c * half + r, tiles[k], t + b)
                put(wa, 1, c * half + r, tiles[k], t - b)

        def compare(k, r):
            for j in range(2):
                fr = zz[k, pl.ds(r, ROWS), tiles[j]]
                fi = zz[k, pl.ds(half + r, ROWS), tiles[j]]
                a = amp_ref[slot, k, pl.ds(r, ROWS), tiles[j]]
                factor = two - two * a * lax.rsqrt(fr * fr + fi * fi + 0.01)
                put(wa, k, r, tiles[j], factor * fr)
                put(wa, k, half + r, tiles[j], factor * fi)

        def turn_back(h, r):
            for k in range(2):
                gr, gi = from_left(h, r, k)
                put(xa, k, h * half + r, tiles[0], gr)
                put(xa, k, h * half + r, tiles[1], gi)

        def grad_late(r):
            pair = []
            for j in range(2):
                grad = []
                for c in range(2):
                    a, b = vv[0, pl.ds(r, ROWS), tiles[c]], vv[1, pl.ds(r, ROWS), tiles[c]]
                    grad.append(a - b if j else a + b)
                gr, gi = grad
                wr, wi = (wave[c, pl.ds(r, ROWS), tiles[j]] for c in range(2))
                add_grad(1, 0, j, r, wr * gr + wi * gi)
                add_grad(1, 1, j, r, wr * gi - wi * gr)
                re, im = (patch(1, c, j, r) for c in range(2))
                pair.append((re * gr + im * gi, re * gi - im * gr))
            put_right(r, *pair)

        def grad_early(h, r):
            row = h * half + r
            terms = ([], [])
            for j in range(2):
                gr, gi = from_left(h, r, j)
                pr, pi = (rolled[c, pl.ds(row, ROWS), tiles[j]] for c in range(2))
                add_grad(0, 0, j, row, pr * gr + pi * gi)
                add_grad(0, 1, j, row, pr * gi - pi * gr)
                re, im = (patch(0, c, j, row) for c in range(2))
                terms[0].append(re * gr + im * gi)
                terms[1].append(re * gi - im * gr)
            for c in range(2):
                term = pltpu.roll(jnp.concatenate(terms[c], axis=1), back, 1)
                probe_grad_ref[c, pl.ds(row, ROWS), :] = probe_grad_ref[c, pl.ds(row, ROWS), :] + term

        pair = range(2)
        return [
            over(start, all_rows),
            right(mat_ref, 0),
            over(turn, upper, pair),
            left_side(matt_ref, 0),
            over(exit_wave, pair, upper),
            right(mat_ref, 2),
            over(turn_far, upper, pair),
            left_side(matt_ref, 2),
            over(compare, pair, upper),
            left_side(mat_ref, 2),
            over(turn_back, pair, upper),
            right(matt_ref, 2),
            over(grad_late, all_rows),
            right(matt_ref, 0),
            over(turn, upper, pair),
            left_side(mat_ref, 0),
            over(grad_early, pair, upper),
        ]

    def visit(step, carry):
        first = 2 * step
        amp_copy(first).wait()
        amp_copy(first + 1).wait()
        live = jnp.where(first + 1 < count, 2.0, 0.0)
        one = phases(0, first, 2.0)
        other = phases(1, jnp.minimum(first + 1, count - 1), live)
        for run in one[0]:
            run()
        for ahead, behind in zip(one[1:], other[:-1]):
            interleave(ahead, behind)
        for run in other[-1]:
            run()
        return carry

    steps = lax.div(count + 1, 2)
    lax.fori_loop(0, steps, visit, 0)

    outer = (pl.ds(0, half), pl.ds(3 * half, half))
    moves = [(gext.at[1:3, :, :, middle, :], core_ref)]
    for j, end, side in ((toward_in, end_in_ref, side_in_ref), (toward_out, end_out_ref, side_out_ref)):
        moves.append((gext.at[j, :, :, middle, :], side))
        for n in range(2):
            moves.append((gext.at[j, :, :, outer[n], :], end.at[n]))
    for n in range(2):
        moves.append((gext.at[1:3, :, :, outer[n], :], slab_ref.at[n]))
    moves = [pltpu.make_async_copy(a, b, out_sems.at[n]) for n, (a, b) in enumerate(moves)]
    for move in moves:
        move.start()

    def leave(slot, carry):
        amp_copy(slot).wait()
        return carry

    lax.fori_loop(2 * steps, 8, leave, 0)
    for move in moves:
        move.wait()


def interleave(first, second):
    at = [((n + 0.5) / len(first), 0, n) for n in range(len(first))]
    at += [((n + 0.5) / len(second), 1, n) for n in range(len(second))]
    for _, which, n in sorted(at):
        (first, second)[which][n]()


def gradients(count, shifts, core, odd, own, row_a, row_b, side_in, side_out, ends_in, ends_out, probe, amps, mats, mats_t):
    width = probe.shape[-1]
    half = width // 2
    shapes = [(2, 2, 2, half, half)] * 2 + [(2, 2, width, half)] * 2 + [(2, 2, 2, 2, half, half), (2, 2, 2, width, half)]
    shapes.append((2, width, width))
    any_space = pl.BlockSpec(memory_space=pl.ANY)
    vmem = pl.BlockSpec(memory_space=pltpu.VMEM)
    smem = pl.BlockSpec(memory_space=pltpu.SMEM)
    return pl.pallas_call(
        main_kernel,
        in_specs=[smem] * 4 + [any_space] * 7 + [vmem] + [any_space] * 3,
        out_specs=[any_space] * 6 + [vmem],
        out_shape=[jax.ShapeDtypeStruct(shape, F32) for shape in shapes],
        scratch_shapes=[
            pltpu.VMEM((4, 2, 2, 4 * half, half), F32),
            pltpu.VMEM((4, 2, 2, 4 * half, half), F32),
            pltpu.VMEM((2, 2, width, width), F32),
            pltpu.VMEM((2, 2, width, width), F32),
            pltpu.VMEM((2, 2, 2, width, width), BF16),
            pltpu.VMEM((2, 2, 2, width, width), BF16),
            pltpu.VMEM((2, 2, width, width), F32),
            pltpu.VMEM((2, 2, width, width), F32),
            pltpu.VMEM((8, 2, half, width), F32),
            pltpu.VMEM((2, 4, width, width), BF16),
            pltpu.VMEM((2, 4, width, width), BF16),
            pltpu.SemaphoreType.DMA((20,)),
            pltpu.SemaphoreType.DMA((8,)),
            pltpu.SemaphoreType.DMA((9,)),
        ],
        cost_estimate=pl.CostEstimate(flops=8 * 48 * 2 * width**3, bytes_accessed=16 << 20, transcendentals=8 * width**2),
        name="slot_gradients",
    )(count, shifts, core, odd, own, row_a, row_b, side_in, side_out, ends_in, ends_out, probe, amps, mats, mats_t)


def edges_kernel(core_at, odd_at, slab_ref, in_ref, out_ref, a_ref, b_ref):
    core, odd = core_at[0], odd_at[0]
    for n, row in ((1 - odd, a_ref), (odd, b_ref)):
        for j, side in ((1 - core, in_ref), (core, out_ref)):
            row[j] = slab_ref[n, j] + side[n]


def merged_edges(core, odd, slabs, end_in, end_out):
    half = slabs.shape[-1]
    smem = pl.BlockSpec(memory_space=pltpu.SMEM)
    ends = pl.BlockSpec((2, 1, 2, half, half), lambda s: (0, s, 0, 0, 0))
    return pl.pallas_call(
        edges_kernel,
        grid=(2,),
        in_specs=[smem, smem, pl.BlockSpec((2, 2, 1, 2, half, half), lambda s: (0, 0, s, 0, 0, 0)), ends, ends],
        out_specs=[ends] * 2,
        out_shape=[jax.ShapeDtypeStruct(slabs.shape[1:], F32)] * 2,
        cost_estimate=pl.CostEstimate(flops=8 * 2 * half**2, bytes_accessed=3 << 20, transcendentals=0),
        compiler_params=pltpu.CompilerParams(vmem_limit_bytes=12 << 20),
        name="merge_edges",
    )(core, odd, slabs, end_in, end_out)


def core_kernel(core_at, odd_at, core_ref, in_ref, out_ref, a_ref, b_ref, grad_ref):
    half = in_ref.shape[-1]
    core, odd = core_at[0], odd_at[0]
    for h, row in ((1 - odd, a_ref), (odd, b_ref)):
        rows = pl.ds(pl.multiple_of(h * half, half), half)
        for j, side in ((1 - core, in_ref), (core, out_ref)):
            cols = pl.ds(pl.multiple_of(j * half, half), half)
            grad_ref[0, :, rows, cols] = core_ref[j, 0, :, rows, :] + side[0, :, rows, :] + row[j, 0]


def merged_core(core, odd, middle, side_in, side_out, row_a, row_b):
    width = middle.shape[3]
    half = width // 2
    smem = pl.BlockSpec(memory_space=pltpu.SMEM)
    side = pl.BlockSpec((1, 2, width, half), lambda s: (s, 0, 0, 0))
    rows = pl.BlockSpec((2, 1, 2, half, half), lambda s: (0, s, 0, 0, 0))
    return pl.pallas_call(
        core_kernel,
        grid=(2,),
        in_specs=[smem, smem, pl.BlockSpec((2, 1, 2, width, half), lambda s: (0, s, 0, 0, 0)), side, side, rows, rows],
        out_specs=pl.BlockSpec((1, 2, width, width), lambda s: (s, 0, 0, 0)),
        out_shape=jax.ShapeDtypeStruct((2, 2, width, width), F32),
        cost_estimate=pl.CostEstimate(flops=8 * width**2, bytes_accessed=4 << 20, transcendentals=0),
        compiler_params=pltpu.CompilerParams(vmem_limit_bytes=12 << 20),
        name="merge_core",
    )(core, odd, middle, side_in, side_out, row_a, row_b)


def swap(value, axis, first):
    pairs = [(n, n + 1) for n in range(first, lax.axis_size(axis) - 1, 2)]
    return lax.ppermute(value, axis, pairs + [(after, before) for before, after in pairs])


def total_over_devices(shard):
    planes, rows, cols = shard.shape
    blocks = shard.reshape(planes, rows // 8, 8, cols // 128, 128).swapaxes(2, 3).reshape(-1, 8, 128)
    parts = lax.all_to_all(blocks, ALL, 0, 0, tiled=True)
    mine = parts.sum(0, keepdims=True)
    whole = lax.all_to_all(jnp.broadcast_to(mine, parts.shape), ALL, 0, 0, tiled=True)
    return whole.reshape(planes, rows // 8, cols // 128, 8, 128).swapaxes(2, 3).reshape(shard.shape)


def by_column(rows):
    half = rows.shape[-1] // 2
    return jnp.stack([rows[..., :half], rows[..., half:]])


def shards(mats, mats_t, object_slices, probe, amplitudes, offsets, counts):
    half = probe.shape[-1] // 2
    core = lax.axis_index(TILE) % 2
    odd = lax.axis_index(POS) % 2
    by_core = (core.reshape(1), odd.reshape(1))

    def pick(where, when_zero, when_one):
        return jnp.where(where == 0, when_zero, when_one)

    top, bottom = by_column(object_slices[:, :, :half]), by_column(object_slices[:, :, half:])
    row_a = swap(pick(odd, bottom, top), POS, 0)
    row_b = swap(pick(odd, top, bottom), POS, 1)
    west, east = object_slices[..., :half], object_slices[..., half:]
    side_in = swap(pick(core, east, west), TILE, 0)
    side_out = swap(pick(core, west, east), TILE, 1)
    ends_out = swap(jnp.stack([pick(core, row_a[0], row_a[1]), pick(core, row_b[0], row_b[1])]), TILE, 1)
    ends_in = swap(jnp.stack([pick(core, row_a[1], row_a[0]), pick(core, row_b[1], row_b[0])]), TILE, 0)
    amps = ordered(amplitudes[0, 0])
    end_in, end_out, grad_in, grad_out, slabs, middle, probe_grad = gradients(
        counts, offsets[0, 0], *by_core, object_slices, row_a, row_b, side_in, side_out, ends_in, ends_out, probe, amps, mats, mats_t
    )
    end_out = swap(end_out, TILE, 1)
    end_in = swap(end_in, TILE, 0)
    grad_out = swap(grad_out, TILE, 1)
    grad_in = swap(grad_in, TILE, 0)
    probe_total = total_over_devices(probe_grad)
    row_a, row_b = merged_edges(*by_core, slabs, end_in, end_out)
    row_a = swap(row_a, POS, 0)
    row_b = swap(row_b, POS, 1)
    object_grad = merged_core(*by_core, middle, grad_in, grad_out, row_a, row_b)
    return (object_grad, probe_total)


def solution(mesh):
    torus = Mesh(mesh.devices.reshape(4, 4, 4, 2), ("pos_0", "pos_1", "tile_0", "tile_1"))
    placed = (
        P(None, None, POS, TILE),
        P(),
        P(POS, TILE, None, None, None),
        P(POS, TILE, None, None),
        P(POS, TILE),
    )
    real = transform_matrices(256)
    mats = jnp.asarray(halves(real))
    mats_t = jnp.asarray(halves(np.swapaxes(real, 1, 2)))
    return jax.shard_map(
        functools.partial(shards, mats, mats_t),
        mesh=torus,
        in_specs=placed,
        out_specs=(P(None, None, POS, TILE), P()),
        check_vma=False,
    )
```

```python
import functools
import itertools
import math

import jax
import jax.numpy as jnp
import numpy as np
from jax import lax
from jax.experimental import pallas as pl
from jax.experimental.pallas import tpu as pltpu
from jax.sharding import Mesh
from jax.sharding import PartitionSpec as P

POS = ("pos_0", "pos_1")
TILE = ("tile_0", "tile_1")
ALL = ("pos_0", "pos_1", "tile_0", "tile_1")
F32 = jnp.float32
BF16 = jnp.bfloat16
ROWS = 32


def real_form(field):
    return np.block([[field.real, field.imag], [-field.imag, field.real]])


def transform_matrices(width):
    half = width // 2
    index = np.arange(width)
    signed = np.where(index < half, index, index - width)
    kernel = np.exp(-1j * 80.0 / (width * width) * signed.astype(np.float64) ** 2)
    impulse = np.fft.ifft(kernel)
    near = np.arange(half)
    gap = (near[:, None] - near[None, :]) % width
    prop_sum = 0.5 * (impulse[gap] + impulse[(gap + half) % width])
    prop_diff = 0.5 * (impulse[gap] - impulse[(gap + half) % width])
    scale = 1.0 / math.sqrt(width)
    even = np.exp(-2j * np.pi / width * (near[:, None] * (2 * near[None, :]) % width)) * scale
    odd = np.exp(-2j * np.pi / width * (near[:, None] * (2 * near[None, :] + 1) % width)) * scale
    return np.stack([real_form(m) for m in (prop_sum, prop_diff, even, odd)])


def halves(matrix):
    high = matrix.astype(np.float32).astype(BF16)
    low = (matrix - high.astype(np.float64)).astype(np.float32).astype(BF16)
    return np.stack([high, low])


def split(value):
    high = value.astype(BF16)
    low = (value - high.astype(F32)).astype(BF16)
    return high, low


def dot(left, right):
    return jnp.dot(left, right, preferred_element_type=F32)


def even_then_odd(width):
    index = np.arange(width)
    source = np.where(index < width // 2, 2 * index, 2 * (index - width // 2) + 1)
    return (index[:, None] == source[None, :]).astype(BF16)


def main_kernel(
    count_ref, shift_ref, core_at, odd_at, own_ref, out_a_ref, out_b_ref, in_a_ref, in_b_ref, side_in_ref, side_out_ref,
    end_in_a_ref, end_in_b_ref, end_out_a_ref, end_out_b_ref, probe_hbm, amps_ref, mats_ref, matts_ref, perms_ref,
    grad_end_in, grad_end_out, grad_side_in, grad_side_out, slab_ref, core_ref, probe_grad_hbm,
    ext, gext, probe_ref, probe_grad_ref, rolleds, waves, xas, was, vvs, zzs, aas, aps, amp_ref, mat_ref, matt_ref, perm_ref, sems, amp_sems, out_sems,
):
    half = 128
    grads = [gext.at[j] for j in range(4)]
    middle = pl.ds(half, 2 * half)
    core, odd = core_at[0], odd_at[0]
    toward_in, toward_out = 3 * (1 - core), 3 * core
    rows_a = pl.ds(pl.multiple_of(3 * half * (1 - odd), half), half)
    rows_b = pl.ds(pl.multiple_of(3 * half * odd, half), half)

    def slice_copies(s):
        pairs = []
        for c in range(2):
            for j in range(2):
                pairs.append((own_ref.at[s, c, :, pl.ds(j * half, half)], ext.at[1 + j, s, c, middle, :]))
        for j, side, ends in (
            (toward_in, side_in_ref, (end_in_a_ref, end_in_b_ref)),
            (toward_out, side_out_ref, (end_out_a_ref, end_out_b_ref)),
            (2 - core, None, (in_a_ref, in_b_ref)),
            (1 + core, None, (out_a_ref, out_b_ref)),
        ):
            if side is not None:
                pairs.append((side.at[s], ext.at[j, s, :, middle, :]))
            pairs.append((ends[0].at[s], ext.at[j, s, :, rows_a, :]))
            pairs.append((ends[1].at[s], ext.at[j, s, :, rows_b, :]))
        return pairs

    early = slice_copies(0) + [(probe_hbm, probe_ref)]
    late = [(mats_ref, mat_ref), (matts_ref, matt_ref), (perms_ref, perm_ref)] + slice_copies(1)
    copies = [pltpu.make_async_copy(a, b, sems.at[n]) for n, (a, b) in enumerate(early + late)]
    for copy in copies:
        copy.start()

    def amp_copies(slot):
        return [
            pltpu.make_async_copy(
                amps_ref.at[slot, :, pl.ds(j * half, half)], amp_ref.at[slot, j], amp_sems.at[slot, j]
            )
            for j in range(2)
        ]

    def wait_amps(slot):
        for copy in amp_copies(slot):
            copy.wait()

    for slot in range(8):
        for copy in amp_copies(slot):
            copy.start()
    gext[...] = jnp.zeros_like(gext)
    probe_grad_ref[...] = jnp.zeros_like(probe_grad_ref)
    for copy in copies[: len(early)]:
        copy.wait()

    lane = lax.broadcasted_iota(jnp.int32, (ROWS, half), 1)
    tiles = (pl.ds(0, half), pl.ds(half, half))
    count = count_ref[0, 0]

    def phases(which, slot, two):
        refs = (rolleds, waves, xas, was, vvs, zzs, aas, aps)
        rolled, wave, xa, wa, vv, zz, aa, ap = (ref.at[which] for ref in refs)
        top = shift_ref[0, slot] + half
        left = shift_ref[1, slot] + half
        back = lax.rem(2 * half - left, 2 * half)
        masks = (lane >= left, lane + half >= left)

        def patch(s, c, j, r):
            rows = pl.ds(top + r, ROWS)
            return jnp.where(masks[j], ext[j, s, c, rows, :], ext[j + 2, s, c, rows, :])

        def add_grad(s, c, j, r, value):
            rows = pl.ds(top + r, ROWS)
            near, far = grads[j], grads[j + 2]
            near[s, c, rows, :] = near[s, c, rows, :] + jnp.where(masks[j], value, 0.0)
            far[s, c, rows, :] = far[s, c, rows, :] + jnp.where(masks[j], 0.0, value)

        def put(ref, k, r, cols, value):
            high, low = split(value)
            ref[0, k, pl.ds(r, ROWS), cols] = high
            ref[1, k, pl.ds(r, ROWS), cols] = low

        def put_right(r, first, second):
            for c in range(2):
                put(xa, 0, r, tiles[c], first[c] + second[c])
                put(xa, 1, r, tiles[c], first[c] - second[c])

        def right(mats, base):
            def piece(k):
                high, low = mats[0, base + k], mats[1, base + k]
                vv[k] = dot(xa[0, k], high) + dot(xa[1, k], high) + dot(xa[0, k], low)

            return [functools.partial(piece, k) for k in range(2)]

        def left_side(mats, base):
            def piece(k):
                high, low = mats[0, base + k], mats[1, base + k]
                zz[k] = dot(high, wa[0, k]) + dot(high, wa[1, k]) + dot(low, wa[0, k])

            return [functools.partial(piece, k) for k in range(2)]

        def over(piece, *ranges):
            return [functools.partial(piece, *at) for at in itertools.product(*ranges)]

        upper = range(0, half, ROWS)
        all_rows = range(0, 2 * half, ROWS)

        def from_left(h, r, j):
            out = []
            for c in range(2):
                a = zz[0, pl.ds(c * half + r, ROWS), tiles[j]]
                b = zz[1, pl.ds(c * half + r, ROWS), tiles[j]]
                out.append(a - b if h else a + b)
            return out

        def start(r):
            for c in range(2):
                rolled[c, pl.ds(r, ROWS), :] = pltpu.roll(probe_ref[c, pl.ds(r, ROWS), :], left, 1)
            pair = []
            for j in range(2):
                pr, pi = (rolled[c, pl.ds(r, ROWS), tiles[j]] for c in range(2))
                re, im = (patch(0, c, j, r) for c in range(2))
                pair.append((pr * re - pi * im, pr * im + pi * re))
            put_right(r, *pair)

        def turn(r, c):
            ts, td = vv[0, pl.ds(r, ROWS), tiles[c]], vv[1, pl.ds(r, ROWS), tiles[c]]
            bs, bd = vv[0, pl.ds(half + r, ROWS), tiles[c]], vv[1, pl.ds(half + r, ROWS), tiles[c]]
            sum_s, sum_d, dif_s, dif_d = ts + bs, td + bd, ts - bs, td - bd
            put(wa, 0, c * half + r, tiles[0], sum_s + sum_d)
            put(wa, 0, c * half + r, tiles[1], sum_s - sum_d)
            put(wa, 1, c * half + r, tiles[0], dif_s + dif_d)
            put(wa, 1, c * half + r, tiles[1], dif_s - dif_d)

        def split_amps(k, r):
            for j in range(2):
                put(aa, k, r, tiles[j], amp_ref[slot, j, pl.ds(2 * r + k, ROWS, stride=2), :])

        def order_amps(k):
            ap[k] = dot(aa[0, k], perm_ref[...]) + dot(aa[1, k], perm_ref[...])

        def exit_wave(h, r):
            row = h * half + r
            pair = []
            for j in range(2):
                wr, wi = from_left(h, r, j)
                wave[0, pl.ds(row, ROWS), tiles[j]] = wr
                wave[1, pl.ds(row, ROWS), tiles[j]] = wi
                re, im = (patch(1, c, j, row) for c in range(2))
                pair.append((wr * re - wi * im, wr * im + wi * re))
            put_right(row, *pair)

        def turn_far(r, c):
            for k in range(2):
                t = vv[k, pl.ds(r, ROWS), tiles[c]]
                b = vv[k, pl.ds(half + r, ROWS), tiles[c]]
                put(wa, 0, c * half + r, tiles[k], t + b)
                put(wa, 1, c * half + r, tiles[k], t - b)

        def compare(k, r):
            for j in range(2):
                fr = zz[k, pl.ds(r, ROWS), tiles[j]]
                fi = zz[k, pl.ds(half + r, ROWS), tiles[j]]
                a = ap[k, pl.ds(r, ROWS), tiles[j]]
                factor = two - two * a * lax.rsqrt(fr * fr + fi * fi + 0.01)
                put(wa, k, r, tiles[j], factor * fr)
                put(wa, k, half + r, tiles[j], factor * fi)

        def turn_back(h, r):
            for k in range(2):
                gr, gi = from_left(h, r, k)
                put(xa, k, h * half + r, tiles[0], gr)
                put(xa, k, h * half + r, tiles[1], gi)

        def grad_late(r):
            pair = []
            for j in range(2):
                grad = []
                for c in range(2):
                    a, b = vv[0, pl.ds(r, ROWS), tiles[c]], vv[1, pl.ds(r, ROWS), tiles[c]]
                    grad.append(a - b if j else a + b)
                gr, gi = grad
                wr, wi = (wave[c, pl.ds(r, ROWS), tiles[j]] for c in range(2))
                add_grad(1, 0, j, r, wr * gr + wi * gi)
                add_grad(1, 1, j, r, wr * gi - wi * gr)
                re, im = (patch(1, c, j, r) for c in range(2))
                pair.append((re * gr + im * gi, re * gi - im * gr))
            put_right(r, *pair)

        def grad_early(h, r):
            row = h * half + r
            terms = ([], [])
            for j in range(2):
                gr, gi = from_left(h, r, j)
                pr, pi = (rolled[c, pl.ds(row, ROWS), tiles[j]] for c in range(2))
                add_grad(0, 0, j, row, pr * gr + pi * gi)
                add_grad(0, 1, j, row, pr * gi - pi * gr)
                re, im = (patch(0, c, j, row) for c in range(2))
                terms[0].append(re * gr + im * gi)
                terms[1].append(re * gi - im * gr)
            for c in range(2):
                term = pltpu.roll(jnp.concatenate(terms[c], axis=1), back, 1)
                probe_grad_ref[c, pl.ds(row, ROWS), :] = probe_grad_ref[c, pl.ds(row, ROWS), :] + term

        pair = range(2)
        return [
            over(start, all_rows),
            right(mat_ref, 0),
            over(turn, upper, pair),
            left_side(matt_ref, 0),
            over(exit_wave, pair, upper),
            right(mat_ref, 2),
            over(turn_far, upper, pair) + over(split_amps, pair, upper),
            left_side(matt_ref, 2) + over(order_amps, pair),
            over(compare, pair, upper),
            left_side(mat_ref, 2),
            over(turn_back, pair, upper),
            right(matt_ref, 2),
            over(grad_late, all_rows),
            right(matt_ref, 0),
            over(turn, upper, pair),
            left_side(mat_ref, 0),
            over(grad_early, pair, upper),
        ]

    def visit(step, carry):
        first = 2 * step
        wait_amps(first)
        wait_amps(first + 1)
        live = jnp.where(first + 1 < count, 2.0, 0.0)
        one = phases(0, first, 2.0)
        other = phases(1, jnp.minimum(first + 1, count - 1), live)
        following = phases(0, jnp.minimum(first + 2, count - 1), 2.0)
        for ahead, behind in zip(one[1:] + following[:1], other):
            interleave(ahead, behind)
        return carry

    for run in phases(0, 0, 2.0)[0]:
        run()
    for copy in copies[len(early) :]:
        copy.wait()
    steps = lax.div(count + 1, 2)
    lax.fori_loop(0, steps, visit, 0)

    outer = (pl.ds(0, half), pl.ds(3 * half, half))
    moves = [(gext.at[1:3, :, :, middle, :], core_ref), (probe_grad_ref, probe_grad_hbm)]
    for j, end, side in ((toward_in, grad_end_in, grad_side_in), (toward_out, grad_end_out, grad_side_out)):
        moves.append((gext.at[j, :, :, middle, :], side))
        for n in range(2):
            moves.append((gext.at[j, :, :, outer[n], :], end.at[n]))
    for n in range(2):
        moves.append((gext.at[1:3, :, :, outer[n], :], slab_ref.at[n]))
    moves = [pltpu.make_async_copy(a, b, out_sems.at[n]) for n, (a, b) in enumerate(moves)]
    for move in moves:
        move.start()

    def leave(slot, carry):
        wait_amps(slot)
        return carry

    lax.fori_loop(2 * steps, 8, leave, 0)
    for move in moves:
        move.wait()


def interleave(first, second):
    at = [((n + 0.5) / len(first), 0, n) for n in range(len(first))]
    at += [((n + 0.5) / len(second), 1, n) for n in range(len(second))]
    for _, which, n in sorted(at):
        (first, second)[which][n]()


def gradients(count, shifts, core, odd, *arrays):
    width = arrays[0].shape[-1]
    half = width // 2
    shapes = [(2, 2, 2, half, half)] * 2 + [(2, 2, width, half)] * 2 + [(2, 2, 2, 2, half, half), (2, 2, 2, width, half)]
    shapes.append((2, width, width))
    any_space = pl.BlockSpec(memory_space=pl.ANY)
    smem = pl.BlockSpec(memory_space=pltpu.SMEM)
    return pl.pallas_call(
        main_kernel,
        in_specs=[smem] * 4 + [any_space] * 16,
        out_specs=[any_space] * 7,
        out_shape=[jax.ShapeDtypeStruct(shape, F32) for shape in shapes],
        scratch_shapes=[
            pltpu.VMEM((4, 2, 2, 4 * half, half), F32),
            pltpu.VMEM((4, 2, 2, 4 * half, half), F32),
            pltpu.VMEM((2, width, width), F32),
            pltpu.VMEM((2, width, width), F32),
            pltpu.VMEM((2, 2, width, width), F32),
            pltpu.VMEM((2, 2, width, width), F32),
            pltpu.VMEM((2, 2, 2, width, width), BF16),
            pltpu.VMEM((2, 2, 2, width, width), BF16),
            pltpu.VMEM((2, 2, width, width), F32),
            pltpu.VMEM((2, 2, width, width), F32),
            pltpu.VMEM((2, 2, 2, half, width), BF16),
            pltpu.VMEM((2, 2, half, width), F32),
            pltpu.VMEM((8, 2, width, half), F32),
            pltpu.VMEM((2, 4, width, width), BF16),
            pltpu.VMEM((2, 4, width, width), BF16),
            pltpu.VMEM((width, width), BF16),
            pltpu.SemaphoreType.DMA((32,)),
            pltpu.SemaphoreType.DMA((8, 2)),
            pltpu.SemaphoreType.DMA((10,)),
        ],
        cost_estimate=pl.CostEstimate(flops=8 * 48 * 2 * width**3, bytes_accessed=16 << 20, transcendentals=8 * width**2),
        name="slot_gradients",
    )(count, shifts, core, odd, *arrays)


def edges_kernel(core_at, odd_at, slab_ref, in_ref, out_ref, a_ref, b_ref):
    core, odd = core_at[0], odd_at[0]
    for n, row in ((1 - odd, a_ref), (odd, b_ref)):
        for j, side in ((1 - core, in_ref), (core, out_ref)):
            row[j] = slab_ref[n, j] + side[n]


def merged_edges(core, odd, slabs, end_in, end_out):
    half = slabs.shape[-1]
    smem = pl.BlockSpec(memory_space=pltpu.SMEM)
    ends = pl.BlockSpec((2, 1, 2, half, half), lambda s: (0, s, 0, 0, 0))
    return pl.pallas_call(
        edges_kernel,
        grid=(2,),
        in_specs=[smem, smem, pl.BlockSpec((2, 2, 1, 2, half, half), lambda s: (0, 0, s, 0, 0, 0)), ends, ends],
        out_specs=[ends] * 2,
        out_shape=[jax.ShapeDtypeStruct(slabs.shape[1:], F32)] * 2,
        cost_estimate=pl.CostEstimate(flops=8 * 2 * half**2, bytes_accessed=3 << 20, transcendentals=0),
        compiler_params=pltpu.CompilerParams(vmem_limit_bytes=12 << 20),
        name="merge_edges",
    )(core, odd, slabs, end_in, end_out)


def core_kernel(core_at, odd_at, core_ref, in_ref, out_ref, a_ref, b_ref, total_ref, grad_ref, probe_ref):
    probe_ref[...] = total_ref[...]
    half = in_ref.shape[-1]
    core, odd = core_at[0], odd_at[0]
    for h, row in ((1 - odd, a_ref), (odd, b_ref)):
        rows = pl.ds(pl.multiple_of(h * half, half), half)
        for j, side in ((1 - core, in_ref), (core, out_ref)):
            cols = pl.ds(pl.multiple_of(j * half, half), half)
            grad_ref[0, :, rows, cols] = core_ref[j, 0, :, rows, :] + side[0, :, rows, :] + row[j, 0]


def merged_core(core, odd, middle, side_in, side_out, row_a, row_b, total):
    width = middle.shape[3]
    half = width // 2
    smem = pl.BlockSpec(memory_space=pltpu.SMEM)
    side = pl.BlockSpec((1, 2, width, half), lambda s: (s, 0, 0, 0))
    rows = pl.BlockSpec((2, 1, 2, half, half), lambda s: (0, s, 0, 0, 0))
    plane = pl.BlockSpec((1, width, width), lambda s: (s, 0, 0))
    return pl.pallas_call(
        core_kernel,
        grid=(2,),
        in_specs=[smem, smem, pl.BlockSpec((2, 1, 2, width, half), lambda s: (0, s, 0, 0, 0)), side, side, rows, rows, plane],
        out_specs=[pl.BlockSpec((1, 2, width, width), lambda s: (s, 0, 0, 0)), plane],
        out_shape=[jax.ShapeDtypeStruct((2, 2, width, width), F32), jax.ShapeDtypeStruct(total.shape, F32)],
        cost_estimate=pl.CostEstimate(flops=8 * width**2, bytes_accessed=4 << 20, transcendentals=0),
        compiler_params=pltpu.CompilerParams(vmem_limit_bytes=12 << 20),
        name="merge_core",
    )(core, odd, middle, side_in, side_out, row_a, row_b, total)


def swap(value, axis, first):
    pairs = [(n, n + 1) for n in range(first, lax.axis_size(axis) - 1, 2)]
    return lax.ppermute(value, axis, pairs + [(after, before) for before, after in pairs])


def total_over_devices(shard):
    planes, rows, cols = shard.shape
    blocks = shard.reshape(planes, rows // 8, 8, cols // 128, 128).swapaxes(2, 3).reshape(-1, 8, 128)
    parts = lax.all_to_all(blocks, ALL, 0, 0, tiled=True)
    mine = parts.sum(0, keepdims=True)
    whole = lax.all_to_all(jnp.broadcast_to(mine, parts.shape), ALL, 0, 0, tiled=True)
    return whole.reshape(planes, rows // 8, cols // 128, 8, 128).swapaxes(2, 3).reshape(shard.shape)


def shards(mats, mats_t, perm, object_slices, probe, amplitudes, offsets, counts):
    half = probe.shape[-1] // 2
    core = lax.axis_index(TILE) % 2
    odd = lax.axis_index(POS) % 2
    by_core = (core.reshape(1), odd.reshape(1))

    def pick(where, when_zero, when_one):
        return jnp.where(where == 0, when_zero, when_one)

    west, east = object_slices[..., :half], object_slices[..., half:]
    outer, inner = pick(core, west, east), pick(core, east, west)

    def rows(columns, other):
        return pick(other, columns[:, :, half:], columns[:, :, :half])

    out_a = swap(rows(outer, odd), POS, 0)
    out_b = swap(rows(outer, 1 - odd), POS, 1)
    side_out = swap(outer, TILE, 1)
    in_a = swap(rows(inner, odd), POS, 0)
    in_b = swap(rows(inner, 1 - odd), POS, 1)
    side_in = swap(inner, TILE, 0)
    end_out_a = swap(out_a, TILE, 1)
    end_out_b = swap(out_b, TILE, 1)
    end_in_a = swap(in_a, TILE, 0)
    end_in_b = swap(in_b, TILE, 0)
    end_in, end_out, grad_in, grad_out, slabs, middle, probe_grad = gradients(
        counts, offsets[0, 0].T, *by_core, object_slices, out_a, out_b, in_a, in_b, side_in, side_out,
        end_in_a, end_in_b, end_out_a, end_out_b, probe, amplitudes[0, 0], mats, mats_t, perm,
    )
    end_out = swap(end_out, TILE, 1)
    end_in = swap(end_in, TILE, 0)
    grad_out = swap(grad_out, TILE, 1)
    grad_in = swap(grad_in, TILE, 0)
    probe_total = total_over_devices(probe_grad)
    row_a, row_b = merged_edges(*by_core, slabs, end_in, end_out)
    row_a = swap(row_a, POS, 0)
    row_b = swap(row_b, POS, 1)
    object_grad, probe_total = merged_core(*by_core, middle, grad_in, grad_out, row_a, row_b, probe_total)
    return (object_grad, probe_total)


def solution(mesh):
    torus = Mesh(mesh.devices.reshape(4, 4, 4, 2), ("pos_0", "pos_1", "tile_0", "tile_1"))
    placed = (
        P(None, None, POS, TILE),
        P(),
        P(POS, TILE, None, None, None),
        P(POS, TILE, None, None),
        P(POS, TILE),
    )
    real = transform_matrices(256)
    mats = jnp.asarray(halves(real))
    mats_t = jnp.asarray(halves(np.swapaxes(real, 1, 2)))
    return jax.shard_map(
        functools.partial(shards, mats, mats_t, jnp.asarray(even_then_odd(256))),
        mesh=torus,
        in_specs=placed,
        out_specs=(P(None, None, POS, TILE), P()),
        check_vma=False,
    )
```
